32 devices in a mesh: dp: 8 (over y, x, core), tensor: 4 (over z).
Axes of the slice: x: 2, y: 2, z: 4, core: 2. Of those that a mesh axis runs over, the one named last changes fastest.
Arguments:
- tokens: bfloat16 [32768, 768], P(('dp', 'tensor')), may hold values from -6 to 6
- segments: int32 [32, 1024], P('dp'), may hold values from 0 to 7, never falling along the last dimension, each value on 1 to 512 neighbouring positions
- w_query: bfloat16 [768, 768], P('dp', 'tensor'), may hold values from -0.21875 to 0.21875
- w_key: bfloat16 [768, 768], P('dp', 'tensor'), may hold values from -0.21875 to 0.21875
- w_value: bfloat16 [768, 768], P('dp', 'tensor'), may hold values from -0.21875 to 0.21875
- w_out: bfloat16 [768, 768], P('tensor', 'dp'), may hold values from -0.875 to 0.875
- w_in: bfloat16 [768, 3072], P('dp', 'tensor'), may hold values from -0.21875 to 0.21875
- w_down: bfloat16 [3072, 768], P('tensor', 'dp'), may hold values from -0.109375 to 0.109375
- b_query: float32 [768], replicated, may hold values from -3 to 3
- b_value: float32 [768], replicated, may hold values from -3 to 3
- b_out: float32 [768], replicated, may hold values from -3 to 3
- b_in: float32 [3072], replicated, may hold values from -3 to 3
- b_down: float32 [768], replicated, may hold values from -3 to 3
- gain_one: float32 [768], replicated, may hold values from 0.5 to 1.5
- shift_one: float32 [768], replicated, may hold values from -3 to 3
- gain_two: float32 [768], replicated, may hold values from 0.5 to 1.5
- shift_two: float32 [768], replicated, may hold values from -3 to 3
- cotangent: bfloat16 [32768, 768], P(('dp', 'tensor')), may hold values from -6 to 6
Outputs:
- layer_out: bfloat16 [32768, 768], P(('dp', 'tensor'))
- input_grad: float32 [32768, 768], P(('dp', 'tensor'))
- grad_w_query: float32 [768, 768], P('dp', 'tensor')
- grad_w_key: float32 [768, 768], P('dp', 'tensor')
- grad_w_value: float32 [768, 768], P('dp', 'tensor')
- grad_w_out: float32 [768, 768], P('tensor', 'dp')
- grad_w_in: float32 [768, 3072], P('dp', 'tensor')
- grad_w_down: float32 [3072, 768], P('tensor', 'dp')
- grad_b_query: float32 [768], replicated
- grad_b_value: float32 [768], replicated
- grad_b_out: float32 [768], replicated
- grad_b_in: float32 [3072], replicated
- grad_b_down: float32 [768], replicated
- grad_gain_one: float32 [768], replicated
- grad_shift_one: float32 [768], replicated
- grad_gain_two: float32 [768], replicated
- grad_shift_two: float32 [768], replicated
The draws below stay inside these ranges and needn't reach their ends.
Inputs may be any that keep to these rules, and one draw needn't show every extreme that they name: `segments`: within a sequence the numbers never fall, so a document's tokens are consecutive; a document has at most 512 tokens, and some document has exactly 512.
All inputs are finite; a program needn't handle non-finite values.
Results may differ from the reference program's by a relative error of at most 0.015.
Values may be sent and summed in bfloat16 or wider, within the bound.
No kernel may reach another device: no remote copies, remote signals or barrier semaphores. Data moves between devices by JAX's collectives and lax.ppermute only.
A program may use at most 192 MiB of HBM per device.

```python
import math
import jax
import jax.numpy as jnp
import numpy as np
from jax import lax

D = 768
H = 12
HD = 64
FF = 3072
L = 1024
SEQ_DP = 4
DOCS = 8
DOC_MOST = 512
SEQUENCES = 32
TOKENS = 32768
N_DP = 8


def spiked(values, own_key, source, target, shards_of, factor):
    def block_of(axis_at):
        return (jnp.arange(values.shape[axis_at]) // (values.shape[axis_at] // shards_of)).reshape((-1,) + (1,) * (values.ndim - 1 - axis_at))

    near = jax.random.permutation(own_key, shards_of)[block_of(target)]
    other_side = (block_of(target) + shards_of // 2) % shards_of
    return jnp.where((block_of(source) == near) | (block_of(source) == other_side), factor * values, values)


def block_levels(rng, shape, split, least, top_value):
    level = 1.0
    for axis_at, shards_of in split:
        heights = jax.random.uniform(jax.random.fold_in(jax.random.fold_in(rng, 6), axis_at), (shards_of,), jnp.float32, least / len(split), top_value / len(split))
        level = level * jnp.repeat(jnp.exp(heights), shape[axis_at] // shards_of).reshape((-1,) + (1,) * (len(shape) - 1 - axis_at))
    return level


def length_profile(amount, total, limit, skew):
    loads = [(1 << 20) // math.isqrt(standing ** skew) + 1 for standing in range(2, amount + 1)]
    rest, holding = total - limit - (amount - 1), [1] * (amount - 1)
    while rest > 0:
        free = [i for i in range(amount - 1) if holding[i] < limit]
        mass, budget = sum([loads[i] for i in free]), rest
        for i in free:
            addition = min(limit - holding[i], max(1, budget * loads[i] // mass), rest)
            holding[i] = holding[i] + addition
            rest = rest - addition
    return np.array([limit] + holding)


def uneven(key, number_of, total, bound, skew):
    if number_of == 2:
        one = jax.random.randint(key, (), max(1, total - bound), min(bound, total - 1) + 1)
        return jnp.stack([one, total - one])
    tallies = jnp.asarray(length_profile(number_of, total, bound, skew), jnp.int32)
    couples = (number_of - 1) // 2
    giver, receiver = tallies[1:1 + 2 * couples:2], tallies[2:2 + 2 * couples:2]
    room = jnp.minimum(giver - 1, bound - receiver)
    shifted = jax.random.randint(jax.random.fold_in(key, 1), (couples,), 0, 1 << 20) % (room + 1)
    tallies = tallies.at[1:1 + 2 * couples:2].set(giver - shifted).at[2:2 + 2 * couples:2].set(receiver + shifted)
    return tallies[jax.random.permutation(jax.random.fold_in(key, 2), number_of)]


def scatter_about(rng, dims, deviation, reach, cuts=(), kind=jnp.bfloat16):
    array = jax.random.normal(rng, dims, jnp.float32) * deviation
    if len(cuts) > 0:
        array = block_levels(rng, dims, cuts, -0.22, 0.18) * array
    return jnp.clip(array, min=-reach, max=reach).astype(kind)


def bell_draw_with(rng, extent, width, bound, shards, heavy, held_as=jnp.bfloat16):
    array = width * jax.random.normal(rng, extent, jnp.float32)
    if shards:
        array = array * block_levels(rng, extent, shards, -0.22, 0.18)
    return jnp.clip(spiked(array, jax.random.fold_in(rng, 3), *heavy), -bound, bound).astype(held_as)


def setup_inputs(seed: int = 0) -> dict:
    key_list = jax.random.split(jax.random.key(seed), 19)
    tokens = bell_draw_with(key_list[0], (TOKENS, D), 1.0, 6.0, ((0, 32),), (0, 1, 32, 2.75))
    segments = jax.vmap(lambda own: jnp.searchsorted(jnp.cumsum(uneven(own, DOCS, L, DOC_MOST, 0)), jnp.arange(L), side="right"))(jax.random.split(key_list[1], SEQUENCES)).reshape((SEQUENCES, L)).astype(jnp.int32)
    w_query = scatter_about(key_list[2], (D, D), D ** -0.5, 0.21875, ((0, 8), (1, 4)))
    w_key = scatter_about(key_list[3], (D, D), D ** -0.5, 0.21875, ((0, 8), (1, 4)))
    w_value = scatter_about(key_list[4], (D, D), D ** -0.5, 0.21875, ((0, 8), (1, 4)))
    w_out = scatter_about(key_list[5], (D, D), (D // 16) ** -0.5, 0.875, ((0, 4), (1, 8)))
    w_in = scatter_about(key_list[6], (D, FF), D ** -0.5, 0.21875, ((0, 8), (1, 4)))
    w_down = scatter_about(key_list[7], (FF, D), FF ** -0.5, 0.109375, ((0, 4), (1, 8)))
    b_query = scatter_about(key_list[8], (D,), 0.3, 3.0, (), jnp.float32)
    b_value = scatter_about(key_list[9], (D,), 0.3, 3.0, (), jnp.float32)
    b_out = scatter_about(key_list[10], (D,), 0.3, 3.0, (), jnp.float32)
    b_in = scatter_about(key_list[11], (FF,), 0.5, 3.0, (), jnp.float32)
    b_down = scatter_about(key_list[12], (D,), 0.3, 3.0, (), jnp.float32)
    gain_one = jnp.clip(1.0 + 0.1 * jax.random.normal(key_list[13], (D,), jnp.float32), 0.5, 1.5)
    shift_one = scatter_about(key_list[14], (D,), 0.3, 3.0, (), jnp.float32)
    gain_two = jnp.clip(1.0 + 0.1 * jax.random.normal(key_list[15], (D,), jnp.float32), 0.5, 1.5)
    shift_two = scatter_about(key_list[16], (D,), 0.3, 3.0, (), jnp.float32)
    cotangent = bell_draw_with(key_list[17], (TOKENS, D), 1.0, 6.0, ((0, 32),), (0, 1, 32, 2.75))
    return dict(tokens=tokens, segments=segments, w_query=w_query, w_key=w_key, w_value=w_value, w_out=w_out, w_in=w_in, w_down=w_down, b_query=b_query, b_value=b_value, b_out=b_out, b_in=b_in, b_down=b_down, gain_one=gain_one, shift_one=shift_one, gain_two=gain_two, shift_two=shift_two, cotangent=cotangent)


@jax.custom_vjp
def low(v):
    return lax.optimization_barrier(v.astype(jnp.bfloat16)).astype(jnp.float32)

@jax.custom_vjp
def low_back(v):
    return v

def low_keep(v):
    return (low(v), None)

def low_pass(kept, grad):
    return (grad,)

def back_keep(v):
    return (v, None)

def back_low(kept, grad):
    return (low(grad),)
low.defvjp(low_keep, low_pass)
low_back.defvjp(back_keep, back_low)
highest = lax.Precision.HIGHEST
epsilon = 1e-06
masked_score = -1e+30

def matmul(left, right):
    return jnp.dot(left, right, precision=highest, preferred_element_type=jnp.float32)

def layer_norm(total, gain, shift):
    average = lax.optimization_barrier(jnp.mean(total, axis=-1, keepdims=True))
    centred = total - average
    spread = lax.optimization_barrier(jnp.mean(centred * centred, axis=-1, keepdims=True))
    return centred * lax.rsqrt(spread + epsilon) * gain + shift

def attend_sequence(item):
    query, keys, values, segment = item
    scores = jnp.einsum('qhd,khd->hqk', query, keys, precision=highest) * HD ** (-0.5)
    scores = low_back(scores)
    same = segment[:, None] == segment[None, :]
    scores = jnp.where(same[None, :, :], scores, masked_score)
    probs = low(jax.nn.softmax(scores, axis=-1))
    return jnp.einsum('hqk,khd->qhd', probs, values, precision=highest)

def block_forward(rows, segment, params):
    w_query, w_key, w_value, w_out, w_in, w_down, b_query, b_value, b_out, b_in, b_down, gain_one, shift_one, gain_two, shift_two = params
    count = segment.shape[0]
    query = low_back(low(matmul(rows, w_query) + b_query))
    keys = low_back(low(matmul(rows, w_key)))
    values = low_back(low(matmul(rows, w_value) + b_value))
    shaped = (query.reshape(count, L, H, HD), keys.reshape(count, L, H, HD), values.reshape(count, L, H, HD), segment)
    mixed = lax.map(jax.checkpoint(attend_sequence), shaped)
    mixed = low_back(low(mixed.reshape(count * L, D)))
    branch = low_back(matmul(mixed, w_out) + b_out)
    first = layer_norm(rows + branch, gain_one, shift_one)
    inner = low_back(matmul(low(first), w_in) + b_in)
    active = low(jax.nn.gelu(inner, approximate=False))
    branch_two = low_back(matmul(active, w_down) + b_down)
    return layer_norm(first + branch_two, gain_two, shift_two)

def reference(tokens, segments, w_query, w_key, w_value, w_out, w_in, w_down, b_query, b_value, b_out, b_in, b_down, gain_one, shift_one, gain_two, shift_two, cotangent):
    params = tuple((item.astype(jnp.float32) for item in (w_query, w_key, w_value, w_out, w_in, w_down, b_query, b_value, b_out, b_in, b_down, gain_one, shift_one, gain_two, shift_two)))
    group = SEQ_DP * L
    all_rows = tokens.astype(jnp.float32).reshape(N_DP, group, D)
    all_segments = segments.reshape(N_DP, SEQ_DP, L)
    all_cotangents = cotangent.astype(jnp.float32).reshape(N_DP, group, D)

    def one_group(totals, item):
        group_rows, group_segments, group_cotangent = item

        def forward(rows_in, params_in):
            return block_forward(rows_in, group_segments, params_in)
        result, pullback = jax.vjp(forward, group_rows, params)
        grad_rows, grad_params = pullback(group_cotangent)
        totals = tuple((left + right for left, right in zip(totals, grad_params)))
        return (totals, (result.astype(jnp.bfloat16), grad_rows))
    zeros = tuple((jnp.zeros_like(item) for item in params))
    totals, (results, grad_rows) = lax.scan(one_group, zeros, (all_rows, all_segments, all_cotangents))
    layer_out = results.reshape(TOKENS, D)
    input_grad = grad_rows.reshape(TOKENS, D)
    return (layer_out, input_grad, totals[0], totals[1], totals[2], totals[3], totals[4], totals[5], totals[6], totals[7], totals[8], totals[9], totals[10], totals[11], totals[12], totals[13], totals[14])
```

```python
import functools

import jax
import jax.numpy as jnp
from jax import lax
from jax.experimental import pallas as pl
from jax.experimental.pallas import tpu as pltpu
from jax.sharding import PartitionSpec as P

D = 768
HD = 64
L = 1024
PAIR = 2 * HD
BLOCK = 256
GRAIN = 128
SIZES = (2, 3, 4, 5, 6, 8)

epsilon = 1e-06
masked_score = -1e30
scale = HD ** (-0.5)
bf16 = jnp.bfloat16
f32 = jnp.float32


def contract(left, right, dims):
    return lax.dot_general(left, right, (dims, ((), ())), preferred_element_type=f32)


def head_lanes(rows, head):
    lane = lax.broadcasted_iota(jnp.int32, (rows, PAIR), 1)
    return (lane // HD) == head


def windows(info_ref, step, body):
    first = info_ref[2 * step]
    need = info_ref[2 * step + 1]
    below = 0
    for size in SIZES:

        @pl.when((need > below) & (need <= size))
        def _():
            start = jnp.minimum(first, L // GRAIN - size) * GRAIN
            body(pl.ds(pl.multiple_of(start, GRAIN), size * GRAIN))

        below = size


def forward_kernel(info_ref, seg_col_ref, seg_row_ref, q_ref, k_ref, v_ref, out_ref):
    def body(window):
        keys = k_ref[window, :]
        values = v_ref[window, :]
        same = seg_col_ref[...] == seg_row_ref[:, window]
        query = q_ref[...] * bf16(scale)
        parts = []
        for head in range(2):
            mine = head_lanes(BLOCK, head)
            scores = contract(jnp.where(mine, query, bf16(0)), keys, ((1,), (1,)))
            scores = jnp.where(same, scores, masked_score)
            top = jnp.max(scores, axis=1, keepdims=True)
            probs = jnp.exp(scores - top)
            total = jnp.sum(probs, axis=1, keepdims=True)
            parts.append(contract(probs.astype(bf16), values, ((1,), (0,))) / total)
        out_ref[...] = jnp.where(head_lanes(BLOCK, 0), parts[0], parts[1]).astype(bf16)

    windows(info_ref, pl.program_id(1), body)


def backward_kernel(
    info_ref, seg_col_ref, seg_row_ref, q_ref, k_ref, v_ref, d_ref, dq_ref, dk_ref, dv_ref, dk_sum, dv_sum
):
    step = pl.program_id(1)

    @pl.when(step == 0)
    def _():
        dk_sum[...] = jnp.zeros_like(dk_sum)
        dv_sum[...] = jnp.zeros_like(dv_sum)

    def body(window):
        keys = k_ref[window, :]
        values = v_ref[window, :]
        same = seg_col_ref[window, :] == seg_row_ref[...]
        query = q_ref[...] * bf16(scale)
        upstream = d_ref[...]
        dq, dk, dv = [], 0.0, 0.0
        for head in range(2):
            mine = head_lanes(BLOCK, head)
            query_h = jnp.where(mine, query, bf16(0))
            upstream_h = jnp.where(mine, upstream, bf16(0))
            scores = contract(keys, query_h, ((1,), (1,)))
            scores = jnp.where(same, scores, masked_score)
            probs = jnp.exp(scores - jnp.max(scores, axis=0, keepdims=True))
            probs = probs * (1.0 / jnp.sum(probs, axis=0, keepdims=True))
            d_probs = contract(values, upstream_h, ((1,), (1,)))
            inner = jnp.sum(probs * d_probs, axis=0, keepdims=True)
            d_scores = (probs * (d_probs - inner)).astype(bf16)
            dk = dk + contract(d_scores, query_h, ((1,), (0,)))
            dv = dv + contract(probs.astype(bf16), upstream_h, ((1,), (0,)))
            dq.append(contract(d_scores, keys, ((0,), (0,))))
        dq_ref[...] = (jnp.where(head_lanes(BLOCK, 0), dq[0], dq[1]) * scale).astype(bf16)
        dk_sum[window, :] += dk
        dv_sum[window, :] += dv

    windows(info_ref, step, body)

    @pl.when(step == pl.num_programs(1) - 1)
    def _():
        dk_ref[...] = dk_sum[...].astype(bf16)
        dv_ref[...] = dv_sum[...].astype(bf16)


def window_info(segment):
    heads_of = segment.reshape(L // BLOCK, BLOCK)
    first = jnp.sum(segment[None, :] < heads_of[:, :1], axis=1)
    last = jnp.sum(segment[None, :] <= heads_of[:, -1:], axis=1)
    begin = first // GRAIN
    need = (last + GRAIN - 1) // GRAIN - begin
    return jnp.stack([begin, need], axis=1).reshape(-1).astype(jnp.int32)


def row_block(column):
    return pl.BlockSpec((BLOCK, PAIR), lambda pair, step, info: (step, pair + column))


def whole_rows(column):
    return pl.BlockSpec((L, PAIR), lambda pair, step, info: (0, pair + column))


def attend_forward(qkv, segment, info):
    pairs = D // PAIR
    return pl.pallas_call(
        forward_kernel,
        out_shape=jax.ShapeDtypeStruct((L, D), bf16),
        grid_spec=pltpu.PrefetchScalarGridSpec(
            num_scalar_prefetch=1,
            grid=(pairs, L // BLOCK),
            in_specs=[
                pl.BlockSpec((BLOCK, 1), lambda pair, step, info: (step, 0)),
                pl.BlockSpec((1, L), lambda pair, step, info: (0, 0)),
                row_block(0),
                whole_rows(pairs),
                whole_rows(2 * pairs),
            ],
            out_specs=row_block(0),
        ),
        name="attend_forward",
    )(info, segment.reshape(L, 1), segment.reshape(1, L), qkv, qkv, qkv)


def attend_backward(qkv, d_mixed, segment, info):
    pairs = D // PAIR
    shape = jax.ShapeDtypeStruct((L, D), bf16)
    return pl.pallas_call(
        backward_kernel,
        out_shape=(shape, shape, shape),
        grid_spec=pltpu.PrefetchScalarGridSpec(
            num_scalar_prefetch=1,
            grid=(pairs, L // BLOCK),
            in_specs=[
                pl.BlockSpec((L, 1), lambda pair, step, info: (0, 0)),
                pl.BlockSpec((1, BLOCK), lambda pair, step, info: (0, step)),
                row_block(0),
                whole_rows(pairs),
                whole_rows(2 * pairs),
                row_block(0),
            ],
            out_specs=(row_block(0), whole_rows(0), whole_rows(0)),
            scratch_shapes=[pltpu.VMEM((L, PAIR), f32), pltpu.VMEM((L, PAIR), f32)],
        ),
        name="attend_backward",
    )(info, segment.reshape(L, 1), segment.reshape(1, L), qkv, qkv, qkv, d_mixed)


def swap(value, axis, size, bit):
    return lax.ppermute(value, axis, [(i, i ^ bit) for i in range(size)])


def shift(value, axis, size, step):
    return lax.ppermute(value, axis, [(i, (i + step) % size) for i in range(size)])


def bits_of(size):
    return [1 << k for k in range(size.bit_length() - 1)]


class Ring:
    def __init__(self, mesh):
        self.dp = mesh.shape["dp"]
        self.tensor = mesh.shape["tensor"]
        self.dp_rank = lax.axis_index("dp")
        self.tensor_rank = lax.axis_index("tensor")

    def outer_bits(self, flip):
        bits = bits_of(self.dp)[1:]
        return bits[::-1] if flip else bits

    def gather_columns(self, shard):
        rows, parts, columns = shard.shape
        full = jnp.zeros((rows, parts, self.tensor, columns), shard.dtype)
        for step in range(self.tensor):
            piece = shard if step == 0 else shift(shard, "tensor", self.tensor, step)
            place = (self.tensor_rank - step) % self.tensor
            full = lax.dynamic_update_slice(full, piece[:, :, None, :], (0, 0, place, 0))
        return full.reshape(rows, parts * self.tensor * columns)

    def gather(self, shard, flip):
        block = self.gather_columns(shard)
        rows, columns = block.shape
        order = self.outer_bits(flip) + [1]
        count = len(order)
        block = block.reshape((1,) * count + (rows, columns))
        for bit in order:
            place = count - 1 - (bit.bit_length() - 1)
            other = swap(block, "dp", self.dp, bit)
            upper = (self.dp_rank & bit) != 0
            block = jnp.concatenate(
                [jnp.where(upper, other, block), jnp.where(upper, block, other)], axis=place
            )
        return block.reshape(self.dp * rows, columns)

    def scatter(self, total, parts, flip):
        rows = total.shape[0] // self.dp
        width = total.shape[1]
        columns = width // (parts * self.tensor)
        order = [1] + self.outer_bits(flip)[::-1]
        count = len(order)
        block = total.reshape((2,) * count + (rows, width))
        for bit in order:
            place = count - 1 - (bit.bit_length() - 1)
            upper = (self.dp_rank & bit) != 0
            low = lax.slice_in_dim(block, 0, 1, axis=place)
            high = lax.slice_in_dim(block, 1, 2, axis=place)
            keep = jnp.where(upper, high, low)
            give = jnp.where(upper, low, high).astype(bf16)
            block = keep.astype(f32) + swap(give, "dp", self.dp, bit).astype(f32)
        block = block.reshape(rows, parts, self.tensor, columns)

        def piece(step):
            place = (self.tensor_rank + step) % self.tensor
            return lax.dynamic_slice(block, (0, 0, place, 0), (rows, parts, 1, columns))[:, :, 0, :]

        result = piece(0)
        for step in range(1, self.tensor):
            result = result + shift(piece(step).astype(bf16), "tensor", self.tensor, step).astype(f32)
        return result

    def total(self, value):
        for bit in bits_of(self.dp):
            value = value + swap(value, "dp", self.dp, bit)
        for bit in bits_of(self.tensor):
            value = value + swap(value, "tensor", self.tensor, bit)
        return value

    def totals(self, values):
        packed = self.total(jnp.concatenate(values).reshape(-1, 128)).reshape(-1)
        parts, start = [], 0
        for value in values:
            parts.append(packed[start : start + value.shape[0]])
            start += value.shape[0]
        return parts


def dot(left, right):
    return jnp.dot(left, right, preferred_element_type=f32)


def dot_right_t(left, right):
    return jnp.einsum("ik,jk->ij", left, right, preferred_element_type=f32)


def dot_left_t(left, right):
    return jnp.einsum("ti,tj->ij", left, right, preferred_element_type=f32)


def norm_forward(total, gain, shift_by):
    average = jnp.mean(total, axis=-1, keepdims=True)
    centred = total - average
    inverse = lax.rsqrt(jnp.mean(centred * centred, axis=-1, keepdims=True) + epsilon)
    normed = centred * inverse
    return (normed * gain + shift_by, normed, inverse)


def norm_backward(upstream, normed, inverse, gain):
    scaled = upstream * gain
    first_term = jnp.mean(scaled, axis=-1, keepdims=True)
    second_term = jnp.mean(scaled * normed, axis=-1, keepdims=True)
    d_total = inverse * (scaled - first_term - normed * second_term)
    return (d_total, jnp.sum(upstream * normed, axis=0), jnp.sum(upstream, axis=0))


def column_sum(value):
    return jnp.sum(value.astype(f32), axis=0)


def on_device(
    mesh,
    tokens,
    segments,
    w_query,
    w_key,
    w_value,
    w_out,
    w_in,
    w_down,
    b_query,
    b_value,
    b_out,
    b_in,
    b_down,
    gain_one,
    shift_one,
    gain_two,
    shift_two,
    cotangent,
):
    ring = Ring(mesh)
    segment = lax.dynamic_slice_in_dim(segments, ring.tensor_rank, 1, 0).reshape(L)
    info = window_info(segment)
    qk_w = ring.gather(jnp.stack([w_query, w_key], axis=1), False)
    vo_w = ring.gather(jnp.stack([w_value, w_out.T], axis=1), True)
    in_w = ring.gather(w_in[:, None, :], False)
    down_t = ring.gather(w_down.T[:, None, :], True)
    value_w = vo_w[:, :D]
    out_t = vo_w[:, D:]

    zero = jnp.zeros_like(b_query)
    qkv_w = jnp.concatenate([qk_w, value_w], axis=1)
    qkv_bias = jnp.concatenate([b_query, zero, b_value])
    qkv = (dot(tokens, qkv_w) + qkv_bias).astype(bf16)
    mixed = attend_forward(qkv, segment, info)
    branch = dot_right_t(mixed, out_t) + b_out
    first, normed_one, inverse_one = norm_forward(tokens.astype(f32) + branch, gain_one, shift_one)
    first_low = first.astype(bf16)
    inner = dot(first_low, in_w) + b_in
    half = 0.5 * (1.0 + lax.erf(inner * (0.5**0.5)))
    active = (inner * half).astype(bf16)
    slope = (half + inner * jnp.exp(-0.5 * inner * inner) * ((0.5 / jnp.pi) ** 0.5)).astype(bf16)
    branch_two = dot_right_t(active, down_t) + b_down
    second, normed_two, inverse_two = norm_forward(first + branch_two, gain_two, shift_two)
    layer_out = second.astype(bf16)

    d_sum_two, grad_gain_two, grad_shift_two = norm_backward(
        cotangent.astype(f32), normed_two, inverse_two, gain_two
    )
    grad_branch_two = d_sum_two.astype(bf16)
    grad_b_down = column_sum(grad_branch_two)
    grad_down = ring.scatter(dot_left_t(grad_branch_two, active), 1, True)
    d_inner = (dot(grad_branch_two, down_t) * slope.astype(f32)).astype(bf16)
    grad_b_in = column_sum(d_inner)
    grad_in = ring.scatter(dot_left_t(first_low, d_inner), 1, False)
    d_first = d_sum_two + dot_right_t(d_inner, in_w)
    d_sum_one, grad_gain_one, grad_shift_one = norm_backward(
        d_first, normed_one, inverse_one, gain_one
    )
    grad_branch = d_sum_one.astype(bf16)
    grad_b_out = column_sum(grad_branch)
    grad_out_full = dot_left_t(grad_branch, mixed)
    d_mixed = dot(grad_branch, out_t).astype(bf16)
    early = ring.totals(
        (grad_b_out, grad_b_in, grad_b_down, grad_gain_one, grad_shift_one, grad_gain_two, grad_shift_two)
    )
    d_query, d_keys, d_values = attend_backward(qkv, d_mixed, segment, info)
    late = ring.totals((column_sum(d_query), column_sum(d_values)))
    grad_qk = ring.scatter(
        jnp.concatenate([dot_left_t(tokens, d_query), dot_left_t(tokens, d_keys)], axis=1), 2, False
    )
    grad_vo = ring.scatter(jnp.concatenate([dot_left_t(tokens, d_values), grad_out_full], axis=1), 2, True)
    d_qkv = jnp.concatenate([d_query, d_keys, d_values], axis=1)
    input_grad = d_sum_one + dot_right_t(d_qkv, qkv_w)

    return (
        layer_out,
        input_grad,
        grad_qk[:, 0],
        grad_qk[:, 1],
        grad_vo[:, 0],
        grad_vo[:, 1].T,
        grad_in[:, 0],
        grad_down[:, 0].T,
        *late,
        *early,
    )


def solution(mesh):
    rows = P(("dp", "tensor"), None)
    wide = P("dp", "tensor")
    tall = P("tensor", "dp")
    vectors = (P(),) * 9
    in_specs = (rows, P("dp", None), wide, wide, wide, tall, wide, tall, *vectors, rows)
    out_specs = (rows, rows, wide, wide, wide, tall, wide, tall, *vectors)
    return jax.shard_map(
        functools.partial(on_device, mesh),
        mesh=mesh,
        in_specs=in_specs,
        out_specs=out_specs,
        check_vma=False,
    )
```

```python
import functools

import jax
import jax.numpy as jnp
from jax import lax
from jax.experimental import pallas as pl
from jax.experimental.pallas import tpu as pltpu
from jax.sharding import PartitionSpec as P

D = 768
HD = 64
L = 1024
PAIR = 2 * HD
BLOCK = 256
GRAIN = 128
SIZES = (2, 3, 4, 5, 6, 8)

epsilon = 1e-06
masked_score = -1e30
scale = HD ** (-0.5)
bf16 = jnp.bfloat16
f32 = jnp.float32


def contract(left, right, dims):
    return lax.dot_general(left, right, (dims, ((), ())), preferred_element_type=f32)


def head_lanes(rows, head):
    lane = lax.broadcasted_iota(jnp.int32, (rows, PAIR), 1)
    return (lane // HD) == head


def windows(info_ref, step, body):
    first = info_ref[2 * step]
    need = info_ref[2 * step + 1]
    below = 0
    for size in SIZES:

        @pl.when((need > below) & (need <= size))
        def _():
            start = jnp.minimum(first, L // GRAIN - size) * GRAIN
            body(pl.ds(pl.multiple_of(start, GRAIN), size * GRAIN))

        below = size


def forward_kernel(info_ref, seg_col_ref, seg_row_ref, q_ref, k_ref, v_ref, out_ref):
    def body(window):
        keys = k_ref[window, :]
        values = v_ref[window, :]
        same = seg_col_ref[...] == seg_row_ref[:, window]
        query = q_ref[...] * bf16(scale)
        parts = []
        for head in range(2):
            mine = head_lanes(BLOCK, head)
            scores = contract(jnp.where(mine, query, bf16(0)), keys, ((1,), (1,)))
            scores = jnp.where(same, scores, masked_score)
            top = jnp.max(scores, axis=1, keepdims=True)
            probs = jnp.exp(scores - top)
            total = jnp.sum(probs, axis=1, keepdims=True)
            parts.append(contract(probs.astype(bf16), values, ((1,), (0,))) / total)
        out_ref[...] = jnp.where(head_lanes(BLOCK, 0), parts[0], parts[1]).astype(bf16)

    windows(info_ref, pl.program_id(1), body)


def backward_kernel(
    info_ref, seg_col_ref, seg_row_ref, q_ref, k_ref, v_ref, d_ref, out_ref, dk_sum, dv_sum
):
    pair = pl.program_id(0)
    step = pl.program_id(1)

    def columns(kind):
        return pl.ds(pl.multiple_of(kind * HALF + pair * PAIR, PAIR), PAIR)

    @pl.when(step == 0)
    def _():
        dk_sum[...] = jnp.zeros_like(dk_sum)
        dv_sum[...] = jnp.zeros_like(dv_sum)

    def body(window):
        keys = k_ref[window, :]
        values = v_ref[window, :]
        same = seg_col_ref[window, :] == seg_row_ref[...]
        query = q_ref[...] * bf16(scale)
        upstream = d_ref[...]
        dq, dk, dv = [], 0.0, 0.0
        for head in range(2):
            mine = head_lanes(BLOCK, head)
            query_h = jnp.where(mine, query, bf16(0))
            upstream_h = jnp.where(mine, upstream, bf16(0))
            scores = contract(keys, query_h, ((1,), (1,)))
            scores = jnp.where(same, scores, masked_score)
            probs = jnp.exp(scores - jnp.max(scores, axis=0, keepdims=True))
            probs = probs * (1.0 / jnp.sum(probs, axis=0, keepdims=True))
            d_probs = contract(values, upstream_h, ((1,), (1,)))
            inner = jnp.sum(probs * d_probs, axis=0, keepdims=True)
            d_scores = (probs * (d_probs - inner)).astype(bf16)
            dk = dk + contract(d_scores, query_h, ((1,), (0,)))
            dv = dv + contract(probs.astype(bf16), upstream_h, ((1,), (0,)))
            dq.append(contract(d_scores, keys, ((0,), (0,))))
        rows = pl.ds(pl.multiple_of(step * BLOCK, BLOCK), BLOCK)
        out_ref[rows, columns(0)] = (jnp.where(head_lanes(BLOCK, 0), dq[0], dq[1]) * scale).astype(bf16)
        dk_sum[window, :] += dk
        dv_sum[window, :] += dv

    windows(info_ref, step, body)

    @pl.when(step == pl.num_programs(1) - 1)
    def _():
        out_ref[:, columns(1)] = dk_sum[...].astype(bf16)
        out_ref[:, columns(2)] = dv_sum[...].astype(bf16)


def window_info(segment):
    heads_of = segment.reshape(L // BLOCK, BLOCK)
    first = jnp.sum(segment[None, :] < heads_of[:, :1], axis=1)
    last = jnp.sum(segment[None, :] <= heads_of[:, -1:], axis=1)
    begin = first // GRAIN
    need = (last + GRAIN - 1) // GRAIN - begin
    return jnp.stack([begin, need], axis=1).reshape(-1).astype(jnp.int32)


PAIRS = D // PAIR
HALF = D // 2
HALF_PAIRS = HALF // PAIR


def column_of(pair, kind):
    return (pair // HALF_PAIRS * 3 + kind) * HALF_PAIRS + pair % HALF_PAIRS


def row_block(kind, base):
    return pl.BlockSpec((BLOCK, PAIR), lambda pair, step, info: (step, column_of(pair + base, kind)))


def whole_rows(kind, base):
    return pl.BlockSpec((L, PAIR), lambda pair, step, info: (0, column_of(pair + base, kind)))


def attend_forward(qkv, segment, info):
    return pl.pallas_call(
        forward_kernel,
        out_shape=jax.ShapeDtypeStruct((L, D), bf16),
        grid_spec=pltpu.PrefetchScalarGridSpec(
            num_scalar_prefetch=1,
            grid=(PAIRS, L // BLOCK),
            in_specs=[
                pl.BlockSpec((BLOCK, 1), lambda pair, step, info: (step, 0)),
                pl.BlockSpec((1, L), lambda pair, step, info: (0, 0)),
                row_block(0, 0),
                whole_rows(1, 0),
                whole_rows(2, 0),
            ],
            out_specs=pl.BlockSpec((BLOCK, PAIR), lambda pair, step, info: (step, pair)),
        ),
        cost_estimate=pl.CostEstimate(flops=26 * 10**9, transcendentals=0, bytes_accessed=8 * 10**6),
        name="attend_forward",
    )(info, segment.reshape(L, 1), segment.reshape(1, L), qkv, qkv, qkv)


def attend_backward(qkv, d_mixed, segment, info, half):
    base = half * HALF_PAIRS
    return pl.pallas_call(
        backward_kernel,
        out_shape=jax.ShapeDtypeStruct((L, 3 * HALF), bf16),
        grid_spec=pltpu.PrefetchScalarGridSpec(
            num_scalar_prefetch=1,
            grid=(HALF_PAIRS, L // BLOCK),
            in_specs=[
                pl.BlockSpec((L, 1), lambda pair, step, info: (0, 0)),
                pl.BlockSpec((1, BLOCK), lambda pair, step, info: (0, step)),
                row_block(0, base),
                whole_rows(1, base),
                whole_rows(2, base),
                pl.BlockSpec((BLOCK, PAIR), lambda pair, step, info: (step, pair + base)),
            ],
            out_specs=pl.BlockSpec((L, 3 * HALF), lambda pair, step, info: (0, 0)),
            scratch_shapes=[pltpu.VMEM((L, PAIR), f32), pltpu.VMEM((L, PAIR), f32)],
        ),
        cost_estimate=pl.CostEstimate(flops=22 * 10**9, transcendentals=0, bytes_accessed=6 * 10**6),
        name="attend_backward",
    )(info, segment.reshape(L, 1), segment.reshape(1, L), qkv, qkv, qkv, d_mixed)


def swap(value, axis, size, bit):
    return lax.ppermute(value, axis, [(i, i ^ bit) for i in range(size)])


def partner(value, axis, size, mask):
    return value if mask == 0 else swap(value, axis, size, mask)


def after(value, *others):
    return lax.optimization_barrier((value, *others))[0]


def bits_of(size):
    return [1 << k for k in range(size.bit_length() - 1)]


class Ring:
    def __init__(self, mesh):
        self.dp = mesh.shape["dp"]
        self.tensor = mesh.shape["tensor"]
        self.dp_rank = lax.axis_index("dp")
        self.tensor_rank = lax.axis_index("tensor")

    def outer_bits(self, flip):
        bits = bits_of(self.dp)[1:]
        return bits[::-1] if flip else bits

    def columns_sent(self, shard):
        return [partner(shard, "tensor", self.tensor, mask) for mask in range(self.tensor)]

    def spread_columns(self, pieces, moves, widths):
        rows = pieces[0].shape[0]

        def kernel(rank_ref, *refs):
            ins, outs = refs[: self.tensor], refs[self.tensor :]
            for rank in range(self.tensor):

                @pl.when(rank_ref[0] == rank)
                def _():
                    for mask in range(self.tensor):
                        for source, width, which, place in moves(rank ^ mask):
                            outs[which][:, place : place + width] = ins[mask][:, source : source + width]

        return pl.pallas_call(
            kernel,
            out_shape=[jax.ShapeDtypeStruct((rows, width), pieces[0].dtype) for width in widths],
            in_specs=[pl.BlockSpec(memory_space=pltpu.SMEM)] + [pl.BlockSpec()] * self.tensor,
            name="spread",
        )(self.tensor_rank.reshape(1), *pieces)

    def pick_columns(self, blocks, moves, width):
        rows = blocks[0].shape[0]

        def kernel(rank_ref, *refs):
            ins, outs = refs[: len(blocks)], refs[len(blocks) :]
            for rank in range(self.tensor):

                @pl.when(rank_ref[0] == rank)
                def _():
                    for mask in range(self.tensor):
                        for source, span, which, place in moves(rank ^ mask):
                            value = ins[which][:, place : place + span]
                            outs[mask][:, source : source + span] = value.astype(outs[mask].dtype)

        return pl.pallas_call(
            kernel,
            out_shape=[
                jax.ShapeDtypeStruct((rows, width), bf16 if mask else f32) for mask in range(self.tensor)
            ],
            in_specs=[pl.BlockSpec(memory_space=pltpu.SMEM)] + [pl.BlockSpec()] * len(blocks),
            name="pick",
        )(self.tensor_rank.reshape(1), *blocks)

    def join(self, block, bit, place, *others):
        other = swap(block, "dp", self.dp, bit)
        if others:
            other = after(other, *others)
        upper = (self.dp_rank & bit) != 0
        return jnp.concatenate(
            [jnp.where(upper, other, block), jnp.where(upper, block, other)], axis=place
        )

    def row_axes(self, block):
        return block.reshape((1,) * len(bits_of(self.dp)) + block.shape)

    def grow(self, block, bits, *others):
        for bit in bits:
            block = self.join(block, bit, len(bits_of(self.dp)) - bit.bit_length(), *others)
        return block

    def rows_of(self, block):
        return block.reshape(-1, block.shape[-1])

    def split(self, block, bit):
        if block.ndim == 2:
            count = len(bits_of(self.dp))
            block = block.reshape((2,) * count + (block.shape[0] // self.dp, block.shape[1]))
        place = block.ndim - 2 - bit.bit_length()
        own = (self.dp_rank // bit) % 2
        keep = lax.dynamic_slice_in_dim(block, own, 1, axis=place)
        give = lax.dynamic_slice_in_dim(block, 1 - own, 1, axis=place).astype(bf16)
        return keep, give, swap(give, "dp", self.dp, bit)

    def received(self, parts, *others):
        got = after(parts[2], *others) if others else parts[2]
        return parts[0] + got.astype(f32)

    def shrink(self, parts, bits, *others):
        for bit in bits:
            parts = self.split(self.received(parts, *others), bit)
        return parts

    def merged(self, parts, *others):
        return self.rows_of(self.received(parts, *others))

    def scatter_columns(self, blocks, moves, width):
        result, *sends = self.pick_columns(blocks, moves, width)
        return [result] + [swap(send, "tensor", self.tensor, mask) for mask, send in enumerate(sends, 1)]

    def added(self, parts, *others):
        parts = lax.optimization_barrier((*parts, *others))[: len(parts)]
        return functools.reduce(lambda left, right: left + right.astype(f32), parts)

    def total(self, value):
        for bit in bits_of(self.dp):
            value = value + swap(value, "dp", self.dp, bit)
        for bit in bits_of(self.tensor):
            value = value + swap(value, "tensor", self.tensor, bit)
        return value

    def totals(self, values):
        packed = self.total(jnp.concatenate(values).reshape(-1, 128)).reshape(-1)
        parts, start = [], 0
        for value in values:
            parts.append(packed[start : start + value.shape[0]])
            start += value.shape[0]
        return parts


def dot(left, right):
    return jnp.dot(left, right, preferred_element_type=f32)


def dot_right_t(left, right):
    return jnp.einsum("ik,jk->ij", left, right, preferred_element_type=f32)


def dot_left_t(left, right):
    return jnp.einsum("ti,tj->ij", left, right, preferred_element_type=f32)


def norm_forward(total, gain, shift_by):
    average = jnp.mean(total, axis=-1, keepdims=True)
    centred = total - average
    inverse = lax.rsqrt(jnp.mean(centred * centred, axis=-1, keepdims=True) + epsilon)
    normed = centred * inverse
    return (normed * gain + shift_by, normed, inverse)


def norm_backward(upstream, normed, inverse, gain):
    scaled = upstream * gain
    first_term = jnp.mean(scaled, axis=-1, keepdims=True)
    second_term = jnp.mean(scaled * normed, axis=-1, keepdims=True)
    d_total = inverse * (scaled - first_term - normed * second_term)
    return (d_total, jnp.sum(upstream * normed, axis=0), jnp.sum(upstream, axis=0))


def column_sum(value):
    return jnp.sum(value.astype(f32), axis=0)


def on_device(
    mesh,
    tokens,
    segments,
    w_query,
    w_key,
    w_value,
    w_out,
    w_in,
    w_down,
    b_query,
    b_value,
    b_out,
    b_in,
    b_down,
    gain_one,
    shift_one,
    gain_two,
    shift_two,
    cotangent,
):
    ring = Ring(mesh)
    segment = lax.dynamic_slice_in_dim(segments, ring.tensor_rank, 1, 0).reshape(L)
    info = window_info(segment)
    head_cols = w_query.shape[1]
    hidden_cols = w_in.shape[1]
    halves = ring.tensor // 2

    def head_moves(rank, kinds=4):
        for kind in range(kinds):
            place = kind * HALF + rank % halves * head_cols
            yield kind * head_cols, head_cols, rank // halves, place

    grad_head_moves = functools.partial(head_moves, kinds=3)

    def hidden_moves(rank):
        for kind in range(2):
            yield kind * hidden_cols, hidden_cols, kind, rank * hidden_cols

    def hidden_grad_moves(rank):
        yield from hidden_moves(rank)
        yield 2 * hidden_cols, head_cols, 2, rank * head_cols

    up, down = ring.outer_bits(False), ring.outer_bits(True)
    head_shard = jnp.concatenate([w_query, w_key, w_value, w_out.T], axis=1)
    low, high = ring.spread_columns(ring.columns_sent(head_shard), head_moves, (4 * HALF, 4 * HALF))
    hidden_shard = after(jnp.concatenate([w_in, w_down.T], axis=1), low, high)
    hidden_pieces = ring.columns_sent(hidden_shard)
    low = ring.grow(ring.row_axes(low), up)
    high = ring.grow(ring.row_axes(high), down)
    hidden_pieces = lax.optimization_barrier((*hidden_pieces, low, high))[: ring.tensor]
    in_part, down_part = ring.spread_columns(hidden_pieces, hidden_moves, (ring.tensor * hidden_cols,) * 2)
    low_w = ring.rows_of(ring.grow(low, [1]))
    high_w = ring.rows_of(ring.grow(high, [1]))
    qkv_w = jnp.concatenate([low_w[:, : 3 * HALF], high_w[:, : 3 * HALF]], axis=1)
    out_t = jnp.concatenate([low_w[:, 3 * HALF :], high_w[:, 3 * HALF :]], axis=1)

    zero = jnp.zeros((HALF,), f32)
    qkv_bias = jnp.concatenate([b_query[:HALF], zero, b_value[:HALF], b_query[HALF:], zero, b_value[HALF:]])
    qkv = (dot(tokens, qkv_w) + qkv_bias).astype(bf16)
    in_part = ring.grow(ring.row_axes(in_part), up[:-1], qkv)
    down_part = ring.grow(ring.row_axes(down_part), down[:-1], qkv)
    qkv = after(qkv, in_part, down_part)
    mixed = attend_forward(qkv, segment, info)
    in_part = ring.grow(in_part, up[-1:], mixed)
    down_part = ring.grow(down_part, down[-1:], mixed)
    mixed = after(mixed, in_part, down_part)
    in_w = ring.rows_of(ring.grow(in_part, [1]))
    down_t = ring.rows_of(ring.grow(down_part, [1]))
    branch = dot_right_t(mixed, out_t) + b_out
    first, normed_one, inverse_one = norm_forward(tokens.astype(f32) + branch, gain_one, shift_one)
    first_low = first.astype(bf16)
    inner = dot(first_low, in_w) + b_in
    half = 0.5 * (1.0 + lax.erf(inner * (0.5**0.5)))
    active = (inner * half).astype(bf16)
    slope = (half + inner * jnp.exp(-0.5 * inner * inner) * ((0.5 / jnp.pi) ** 0.5)).astype(bf16)
    active, slope = lax.optimization_barrier((active, slope))
    branch_two = dot_right_t(active, down_t) + b_down
    second, normed_two, inverse_two = norm_forward(first + branch_two, gain_two, shift_two)
    layer_out = second.astype(bf16)

    d_sum_two, grad_gain_two, grad_shift_two = norm_backward(
        cotangent.astype(f32), normed_two, inverse_two, gain_two
    )
    grad_branch_two = d_sum_two.astype(bf16)
    grad_b_down = column_sum(grad_branch_two)
    up, down = up[::-1], down[::-1]
    down_grad = ring.split(dot_left_t(grad_branch_two, active), 1)
    grad_branch_two = after(grad_branch_two, down_grad[1])
    d_inner = (dot(grad_branch_two, down_t) * slope.astype(f32)).astype(bf16)
    grad_b_in = column_sum(d_inner)
    down_grad = ring.shrink(down_grad, down[:-1])
    d_inner = after(d_inner, down_grad[1])
    in_grad = ring.split(dot_left_t(first_low, d_inner), 1)
    d_inner = after(d_inner, in_grad[1])
    d_first = d_sum_two + dot_right_t(d_inner, in_w)
    d_sum_one, grad_gain_one, grad_shift_one = norm_backward(
        d_first, normed_one, inverse_one, gain_one
    )
    grad_branch = d_sum_one.astype(bf16)
    grad_b_out = column_sum(grad_branch)
    in_grad = ring.shrink(in_grad, up[:-1])
    grad_branch = after(grad_branch, in_grad[1])
    out_grad = ring.split(dot_left_t(grad_branch, mixed), 1)
    grad_branch = after(grad_branch, out_grad[1])
    d_mixed = dot(grad_branch, out_t).astype(bf16)
    d_low = attend_backward(qkv, d_mixed, segment, info, 0)
    down_grad = ring.shrink(down_grad, down[-1:], d_low)
    in_grad = ring.shrink(in_grad, up[-1:], d_low)
    d_low = after(d_low, down_grad[1], in_grad[1])
    low_grad = ring.split(dot_left_t(tokens, d_low), 1)
    out_grad = ring.shrink(out_grad, up[:-1], d_low)
    d_mixed = after(d_mixed, out_grad[1], low_grad[1])
    d_high = attend_backward(qkv, d_mixed, segment, info, 1)
    high_grad = ring.split(dot_left_t(tokens, d_high), 1)
    low_grad = ring.shrink(low_grad, up[:-1], high_grad[1])
    out_grad = ring.shrink(out_grad, up[-1:], high_grad[1])
    hidden = [ring.merged(part, low_grad[1]) for part in (in_grad, down_grad)]
    high_grad = ring.shrink(high_grad, down[:1], *hidden)
    hidden.append(ring.merged(out_grad, high_grad[1]))
    hidden_parts = ring.scatter_columns(hidden, hidden_grad_moves, 2 * hidden_cols + head_cols)
    d_qkv = jnp.concatenate([d_low, d_high], axis=1)
    d_qkv = after(d_qkv, *hidden_parts[:1])
    input_grad = d_sum_one + dot_right_t(d_qkv, qkv_w)
    low_grad = ring.shrink(low_grad, up[-1:])
    high_grad = ring.shrink(high_grad, down[1:])
    head_parts = ring.scatter_columns(
        (ring.merged(low_grad), ring.merged(high_grad)), grad_head_moves, 3 * head_cols
    )
    grad_hidden = ring.added(hidden_parts, *head_parts[:1])
    grad_head = ring.added(head_parts)
    sums = column_sum(d_qkv)
    vectors = ring.totals(
        (
            jnp.concatenate([sums[:HALF], sums[3 * HALF : 4 * HALF]]),
            jnp.concatenate([sums[2 * HALF : 3 * HALF], sums[5 * HALF :]]),
            grad_b_out,
            grad_b_in,
            grad_b_down,
            grad_gain_one,
            grad_shift_one,
            grad_gain_two,
            grad_shift_two,
        )
    )
    return (
        layer_out,
        input_grad,
        grad_head[:, :head_cols],
        grad_head[:, head_cols : 2 * head_cols],
        grad_head[:, 2 * head_cols : 3 * head_cols],
        grad_hidden[:, 2 * hidden_cols :].T,
        grad_hidden[:, :hidden_cols],
        grad_hidden[:, hidden_cols : 2 * hidden_cols].T,
        *vectors,
    )


def solution(mesh):
    rows = P(("dp", "tensor"), None)
    wide = P("dp", "tensor")
    tall = P("tensor", "dp")
    vectors = (P(),) * 9
    in_specs = (rows, P("dp", None), wide, wide, wide, tall, wide, tall, *vectors, rows)
    out_specs = (rows, rows, wide, wide, wide, tall, wide, tall, *vectors)
    return jax.shard_map(
        functools.partial(on_device, mesh),
        mesh=mesh,
        in_specs=in_specs,
        out_specs=out_specs,
        check_vma=False,
    )
```

```python
import functools

import jax
import jax.numpy as jnp
from jax import lax
from jax.experimental import pallas as pl
from jax.experimental.pallas import tpu as pltpu
from jax.sharding import PartitionSpec as P

D = 768
HD = 64
L = 1024
PAIR = 2 * HD
BLOCK = 256
GRAIN = 128
SIZES = (2, 3, 4, 5, 6, 8)

epsilon = 1e-06
masked_score = -1e30
scale = HD ** (-0.5)
bf16 = jnp.bfloat16
f32 = jnp.float32


def contract(left, right, dims):
    return lax.dot_general(left, right, (dims, ((), ())), preferred_element_type=f32)


def head_lanes(rows, head):
    lane = lax.broadcasted_iota(jnp.int32, (rows, PAIR), 1)
    return (lane // HD) == head


def windows(info_ref, step, body):
    first = info_ref[2 * step]
    need = info_ref[2 * step + 1]
    below = 0
    for size in SIZES:

        @pl.when((need > below) & (need <= size))
        def _():
            start = jnp.minimum(first, L // GRAIN - size) * GRAIN
            body(pl.ds(pl.multiple_of(start, GRAIN), size * GRAIN))

        below = size


def lanes(start):
    return pl.ds(pl.multiple_of(start, PAIR), PAIR)


def stacked(rows):
    zero = jnp.zeros_like(rows)
    return jnp.concatenate(
        [jnp.where(head_lanes(BLOCK, 0), rows, zero), jnp.where(head_lanes(BLOCK, 1), rows, zero)], axis=0
    )


def unstacked(rows):
    return jnp.where(head_lanes(BLOCK, 0), rows[:BLOCK], rows[BLOCK:])


def forward_kernel(info_ref, seg_col_ref, seg_row_ref, qkv_ref, out_ref):
    step = pl.program_id(0)
    rows = pl.ds(pl.multiple_of(step * BLOCK, BLOCK), BLOCK)

    def body(window):
        same = seg_col_ref[...] == seg_row_ref[:, window]
        bias = jnp.where(same, 0.0, masked_score)
        bias = jnp.concatenate([bias, bias], axis=0)

        def one_pair(pair, _):
            base = (pair // HALF_PAIRS * 3 * HALF_PAIRS + pair % HALF_PAIRS) * PAIR
            query = stacked(qkv_ref[rows, lanes(base)] * bf16(scale))
            keys = qkv_ref[window, lanes(base + HALF)]
            values = qkv_ref[window, lanes(base + 2 * HALF)]
            scores = contract(query, keys, ((1,), (1,))) + bias
            top = jnp.max(scores, axis=1, keepdims=True)
            probs = jnp.exp(scores - top)
            total = jnp.sum(probs, axis=1, keepdims=True)
            mixed = contract(probs.astype(bf16), values, ((1,), (0,))) / total
            out_ref[:, lanes(pair * PAIR)] = unstacked(mixed).astype(bf16)
            return 0

        lax.fori_loop(0, PAIRS, one_pair, 0)

    windows(info_ref, step, body)


def backward_kernel(base, info_ref, seg_col_ref, seg_row_ref, qkv_ref, d_ref, out_ref, dk_sum, dv_sum):
    step = pl.program_id(0)
    rows = pl.ds(pl.multiple_of(step * BLOCK, BLOCK), BLOCK)

    @pl.when(step == 0)
    def _():
        dk_sum[...] = jnp.zeros_like(dk_sum)
        dv_sum[...] = jnp.zeros_like(dv_sum)

    def body(window):
        same = seg_col_ref[window, :] == seg_row_ref[...]
        bias = jnp.where(same, 0.0, masked_score)
        bias = jnp.concatenate([bias, bias], axis=1)

        def one_pair(pair, _):
            query = stacked(qkv_ref[rows, lanes(3 * base + pair * PAIR)] * bf16(scale))
            keys = qkv_ref[window, lanes(3 * base + HALF + pair * PAIR)]
            values = qkv_ref[window, lanes(3 * base + 2 * HALF + pair * PAIR)]
            upstream = stacked(d_ref[:, lanes(base + pair * PAIR)])
            scores = contract(keys, query, ((1,), (1,))) + bias
            probs = jnp.exp(scores - jnp.max(scores, axis=0, keepdims=True))
            probs = probs * (1.0 / jnp.sum(probs, axis=0, keepdims=True))
            d_probs = contract(values, upstream, ((1,), (1,)))
            inner = jnp.sum(probs * d_probs, axis=0, keepdims=True)
            d_scores = (probs * (d_probs - inner)).astype(bf16)
            here = lanes(pair * PAIR)
            dk_sum[window, here] += contract(d_scores, query, ((1,), (0,)))
            dv_sum[window, here] += contract(probs.astype(bf16), upstream, ((1,), (0,)))
            dq = contract(d_scores, keys, ((0,), (0,)))
            out_ref[rows, here] = (unstacked(dq) * scale).astype(bf16)
            return 0

        lax.fori_loop(0, HALF_PAIRS, one_pair, 0)

    windows(info_ref, step, body)

    @pl.when(step == pl.num_programs(0) - 1)
    def _():
        out_ref[:, HALF : 2 * HALF] = dk_sum[...].astype(bf16)
        out_ref[:, 2 * HALF :] = dv_sum[...].astype(bf16)


def window_info(segment):
    heads_of = segment.reshape(L // BLOCK, BLOCK)
    first = jnp.sum(segment[None, :] < heads_of[:, :1], axis=1)
    last = jnp.sum(segment[None, :] <= heads_of[:, -1:], axis=1)
    begin = first // GRAIN
    need = (last + GRAIN - 1) // GRAIN - begin
    return jnp.stack([begin, need], axis=1).reshape(-1).astype(jnp.int32)


PAIRS = D // PAIR
HALF = D // 2
HALF_PAIRS = HALF // PAIR


def attend_forward(qkv, segment, info):
    return pl.pallas_call(
        forward_kernel,
        out_shape=jax.ShapeDtypeStruct((L, D), bf16),
        grid_spec=pltpu.PrefetchScalarGridSpec(
            num_scalar_prefetch=1,
            grid=(L // BLOCK,),
            in_specs=[
                pl.BlockSpec((BLOCK, 1), lambda step, info: (step, 0)),
                pl.BlockSpec((1, L), lambda step, info: (0, 0)),
                pl.BlockSpec((L, 3 * D), lambda step, info: (0, 0)),
            ],
            out_specs=pl.BlockSpec((BLOCK, D), lambda step, info: (step, 0)),
        ),
        cost_estimate=pl.CostEstimate(flops=26 * 10**9, transcendentals=0, bytes_accessed=8 * 10**6),
        name="attend_forward",
    )(info, segment.reshape(L, 1), segment.reshape(1, L), qkv)


def attend_backward(qkv, d_mixed, segment, info, half):
    return pl.pallas_call(
        functools.partial(backward_kernel, half * HALF),
        out_shape=jax.ShapeDtypeStruct((L, 3 * HALF), bf16),
        grid_spec=pltpu.PrefetchScalarGridSpec(
            num_scalar_prefetch=1,
            grid=(L // BLOCK,),
            in_specs=[
                pl.BlockSpec((L, 1), lambda step, info: (0, 0)),
                pl.BlockSpec((1, BLOCK), lambda step, info: (0, step)),
                pl.BlockSpec((L, 3 * D), lambda step, info: (0, 0)),
                pl.BlockSpec((BLOCK, D), lambda step, info: (step, 0)),
            ],
            out_specs=pl.BlockSpec((L, 3 * HALF), lambda step, info: (0, 0)),
            scratch_shapes=[pltpu.VMEM((L, HALF), f32), pltpu.VMEM((L, HALF), f32)],
        ),
        cost_estimate=pl.CostEstimate(flops=22 * 10**9, transcendentals=0, bytes_accessed=6 * 10**6),
        name="attend_backward",
    )(info, segment.reshape(L, 1), segment.reshape(1, L), qkv, d_mixed)


def swap(value, axis, size, bit):
    return lax.ppermute(value, axis, [(i, i ^ bit) for i in range(size)])


def partner(value, axis, size, mask):
    return value if mask == 0 else swap(value, axis, size, mask)


def after(value, *others):
    return lax.optimization_barrier((value, *others))[0]


def bits_of(size):
    return [1 << k for k in range(size.bit_length() - 1)]


class Ring:
    def __init__(self, mesh):
        self.dp = mesh.shape["dp"]
        self.tensor = mesh.shape["tensor"]
        self.dp_rank = lax.axis_index("dp")
        self.tensor_rank = lax.axis_index("tensor")

    def outer_bits(self, flip):
        bits = bits_of(self.dp)[1:]
        return bits[::-1] if flip else bits

    def columns_sent(self, shard):
        return [partner(shard, "tensor", self.tensor, mask) for mask in range(self.tensor)]

    def spread_columns(self, pieces, moves, widths):
        rows = pieces[0].shape[0]

        def kernel(rank_ref, *refs):
            ins, outs = refs[: self.tensor], refs[self.tensor :]
            for rank in range(self.tensor):

                @pl.when(rank_ref[0] == rank)
                def _():
                    for mask in range(self.tensor):
                        for source, width, which, place in moves(rank ^ mask):
                            outs[which][:, place : place + width] = ins[mask][:, source : source + width]

        return pl.pallas_call(
            kernel,
            out_shape=[jax.ShapeDtypeStruct((rows, width), pieces[0].dtype) for width in widths],
            in_specs=[pl.BlockSpec(memory_space=pltpu.SMEM)] + [pl.BlockSpec()] * self.tensor,
            name="spread",
        )(self.tensor_rank.reshape(1), *pieces)

    def pick_columns(self, blocks, moves, width):
        rows = blocks[0].shape[0]

        def kernel(rank_ref, *refs):
            ins, outs = refs[: len(blocks)], refs[len(blocks) :]
            for rank in range(self.tensor):

                @pl.when(rank_ref[0] == rank)
                def _():
                    for mask in range(self.tensor):
                        for source, span, which, place in moves(rank ^ mask):
                            value = ins[which][:, place : place + span]
                            outs[mask][:, source : source + span] = value.astype(outs[mask].dtype)

        return pl.pallas_call(
            kernel,
            out_shape=[
                jax.ShapeDtypeStruct((rows, width), bf16 if mask else f32) for mask in range(self.tensor)
            ],
            in_specs=[pl.BlockSpec(memory_space=pltpu.SMEM)] + [pl.BlockSpec()] * len(blocks),
            name="pick",
        )(self.tensor_rank.reshape(1), *blocks)

    def join(self, block, bit, place, *others):
        other = swap(block, "dp", self.dp, bit)
        if others:
            other = after(other, *others)
        upper = (self.dp_rank & bit) != 0
        return jnp.concatenate(
            [jnp.where(upper, other, block), jnp.where(upper, block, other)], axis=place
        )

    def row_axes(self, block):
        return block.reshape((1,) * len(bits_of(self.dp)) + block.shape)

    def grow(self, block, bits, *others):
        for bit in bits:
            block = self.join(block, bit, len(bits_of(self.dp)) - bit.bit_length(), *others)
        return block

    def rows_of(self, block):
        return block.reshape(-1, block.shape[-1])

    def split(self, block, bit):
        if block.ndim == 2:
            count = len(bits_of(self.dp))
            block = block.reshape((2,) * count + (block.shape[0] // self.dp, block.shape[1]))
        place = block.ndim - 2 - bit.bit_length()
        own = (self.dp_rank // bit) % 2
        keep = lax.dynamic_slice_in_dim(block, own, 1, axis=place).astype(f32)
        give = lax.dynamic_slice_in_dim(block, 1 - own, 1, axis=place).astype(bf16)
        return keep, give, swap(give, "dp", self.dp, bit)

    def received(self, parts, *others):
        got = after(parts[2], *others) if others else parts[2]
        return parts[0] + got.astype(f32)

    def shrink(self, parts, bits, *others):
        for bit in bits:
            parts = self.split(self.received(parts, *others), bit)
        return parts

    def merged(self, parts, *others):
        return self.rows_of(self.received(parts, *others))

    def scatter_columns(self, blocks, moves, width):
        result, *sends = self.pick_columns(blocks, moves, width)
        return [result] + [swap(send, "tensor", self.tensor, mask) for mask, send in enumerate(sends, 1)]

    def added(self, parts, *others):
        parts = lax.optimization_barrier((*parts, *others))[: len(parts)]
        return functools.reduce(lambda left, right: left + right.astype(f32), parts)

    def summed(self, value, axis, masks, *others):
        parts = [partner(value, axis, getattr(self, axis), mask) for mask in masks]
        parts = lax.optimization_barrier((*parts, *others))[: len(parts)]
        while len(parts) > 1:
            parts = [left + right for left, right in zip(parts[::2], parts[1::2])]
        return parts[0]


def pack(vectors):
    total = sum(vector.shape[0] for vector in vectors)

    def kernel(*refs):
        row = 0
        for ref in refs[:-1]:
            for start in range(0, ref.shape[1], 128):
                refs[-1][row : row + 1, :] = ref[:, start : start + 128]
                row += 1

    return pl.pallas_call(
        kernel, out_shape=jax.ShapeDtypeStruct((total // 128, 128), f32), name="pack"
    )(*[vector.reshape(1, -1) for vector in vectors])


def unpacked(packed, lengths):
    packed, parts, start = packed.reshape(-1), [], 0
    for length in lengths:
        parts.append(packed[start : start + length])
        start += length
    return parts


def dot(left, right):
    return jnp.dot(left, right, preferred_element_type=f32)


def dot_right_t(left, right):
    return jnp.einsum("ik,jk->ij", left, right, preferred_element_type=f32)


def weight_grad(left, right):
    return jnp.einsum("ti,tj->ij", left, right, preferred_element_type=f32).astype(bf16)


def norm_forward(total, gain, shift_by):
    average = jnp.mean(total, axis=-1, keepdims=True)
    centred = total - average
    inverse = lax.rsqrt(jnp.mean(centred * centred, axis=-1, keepdims=True) + epsilon)
    normed = centred * inverse
    return (normed * gain + shift_by, normed, inverse)


def norm_backward(upstream, normed, inverse, gain):
    scaled = upstream * gain
    first_term = jnp.mean(scaled, axis=-1, keepdims=True)
    second_term = jnp.mean(scaled * normed, axis=-1, keepdims=True)
    d_total = inverse * (scaled - first_term - normed * second_term)
    return (d_total, jnp.sum(upstream * normed, axis=0), jnp.sum(upstream, axis=0))


def column_sum(value):
    return jnp.sum(value.astype(f32), axis=0)


def on_device(
    mesh,
    tokens,
    segments,
    w_query,
    w_key,
    w_value,
    w_out,
    w_in,
    w_down,
    b_query,
    b_value,
    b_out,
    b_in,
    b_down,
    gain_one,
    shift_one,
    gain_two,
    shift_two,
    cotangent,
):
    ring = Ring(mesh)
    segment = lax.dynamic_slice_in_dim(segments, ring.tensor_rank, 1, 0).reshape(L)
    info = window_info(segment)
    head_cols = w_query.shape[1]
    hidden_cols = w_in.shape[1]
    halves = ring.tensor // 2

    def head_moves(rank, kinds=4):
        for kind in range(kinds):
            place = kind * HALF + rank % halves * head_cols
            yield kind * head_cols, head_cols, rank // halves, place

    grad_head_moves = functools.partial(head_moves, kinds=3)

    def hidden_moves(rank):
        for kind in range(2):
            yield kind * hidden_cols, hidden_cols, kind, rank * hidden_cols

    def hidden_grad_moves(rank):
        yield from hidden_moves(rank)
        yield 2 * hidden_cols, head_cols, 2, rank * head_cols

    up, down = ring.outer_bits(False), ring.outer_bits(True)
    head_shard = jnp.concatenate([w_query, w_key, w_value, w_out.T], axis=1)
    low, high = ring.spread_columns(ring.columns_sent(head_shard), head_moves, (4 * HALF, 4 * HALF))
    hidden_shard = after(jnp.concatenate([w_in, w_down.T], axis=1), low, high)
    hidden_pieces = ring.columns_sent(hidden_shard)
    low = ring.grow(ring.row_axes(low), up[:-1], hidden_pieces[1])
    high = ring.grow(ring.row_axes(high), down[:-1], hidden_pieces[1])
    low = ring.grow(low, up[-1:], *hidden_pieces[2:])
    high = ring.grow(high, down[-1:], *hidden_pieces[2:])
    in_part, down_part = ring.spread_columns(hidden_pieces, hidden_moves, (ring.tensor * hidden_cols,) * 2)
    low_w = ring.rows_of(ring.grow(low, [1], in_part, down_part))
    high_w = ring.rows_of(ring.grow(high, [1], in_part, down_part))
    qkv_w = jnp.concatenate([low_w[:, : 3 * HALF], high_w[:, : 3 * HALF]], axis=1)
    out_t = jnp.concatenate([low_w[:, 3 * HALF :], high_w[:, 3 * HALF :]], axis=1)

    zero = jnp.zeros((HALF,), f32)
    qkv_bias = jnp.concatenate([b_query[:HALF], zero, b_value[:HALF], b_query[HALF:], zero, b_value[HALF:]])
    qkv = (dot(tokens, qkv_w) + qkv_bias).astype(bf16)
    in_part = ring.grow(ring.row_axes(in_part), up[:-1], qkv)
    down_part = ring.grow(ring.row_axes(down_part), down[:-1], qkv)
    qkv = after(qkv, in_part, down_part)
    mixed = attend_forward(qkv, segment, info)
    in_part = ring.grow(in_part, up[-1:], mixed)
    down_part = ring.grow(down_part, down[-1:], mixed)
    mixed = after(mixed, in_part, down_part)
    in_w = ring.rows_of(ring.grow(in_part, [1]))
    down_t = ring.rows_of(ring.grow(down_part, [1]))
    branch = dot_right_t(mixed, out_t) + b_out
    first, normed_one, inverse_one = norm_forward(tokens.astype(f32) + branch, gain_one, shift_one)
    first_low = first.astype(bf16)
    inner = dot(first_low, in_w) + b_in
    half = 0.5 * (1.0 + lax.erf(inner * (0.5**0.5)))
    active = (inner * half).astype(bf16)
    slope = (half + inner * jnp.exp(-0.5 * inner * inner) * ((0.5 / jnp.pi) ** 0.5)).astype(bf16)
    active, slope = lax.optimization_barrier((active, slope))
    branch_two = dot_right_t(active, down_t) + b_down
    second, normed_two, inverse_two = norm_forward(first + branch_two, gain_two, shift_two)
    layer_out = second.astype(bf16)

    d_sum_two, grad_gain_two, grad_shift_two = norm_backward(
        cotangent.astype(f32), normed_two, inverse_two, gain_two
    )
    grad_branch_two = d_sum_two.astype(bf16)
    grad_b_down = column_sum(grad_branch_two)
    up, down = up[::-1], down[::-1]
    down_grad = ring.split(weight_grad(grad_branch_two, active), 1)
    grad_branch_two = after(grad_branch_two, down_grad[1])
    d_inner = (dot(grad_branch_two, down_t) * slope.astype(f32)).astype(bf16)
    grad_b_in = column_sum(d_inner)
    down_grad = ring.shrink(down_grad, down[:-1])
    d_inner = after(d_inner, down_grad[1])
    in_grad = ring.split(weight_grad(first_low, d_inner), 1)
    d_inner = after(d_inner, in_grad[1])
    d_first = d_sum_two + dot_right_t(d_inner, in_w)
    d_sum_one, grad_gain_one, grad_shift_one = norm_backward(
        d_first, normed_one, inverse_one, gain_one
    )
    grad_branch = d_sum_one.astype(bf16)
    grad_b_out = column_sum(grad_branch)
    in_grad = ring.shrink(in_grad, up[:-1])
    grad_branch = after(grad_branch, in_grad[1])
    out_grad = ring.split(weight_grad(grad_branch, mixed), 1)
    grad_branch = after(grad_branch, out_grad[1])
    d_mixed = dot(grad_branch, out_t).astype(bf16)
    d_low = attend_backward(qkv, d_mixed, segment, info, 0)
    down_grad = ring.shrink(down_grad, down[-1:], d_low)
    in_grad = ring.shrink(in_grad, up[-1:], d_low)
    d_low = after(d_low, down_grad[1], in_grad[1])
    low_grad = ring.split(weight_grad(tokens, d_low), 1)
    out_grad = ring.shrink(out_grad, up[:-1], d_low)
    d_mixed = after(d_mixed, out_grad[1], low_grad[1])
    d_high = attend_backward(qkv, d_mixed, segment, info, 1)
    high_grad = ring.split(weight_grad(tokens, d_high), 1)
    low_grad = ring.shrink(low_grad, up[:-1], high_grad[1])
    out_grad = ring.shrink(out_grad, up[-1:], high_grad[1])
    high_grad = ring.shrink(high_grad, down[:1])
    d_qkv = jnp.concatenate([d_low, d_high], axis=1)
    sums = column_sum(d_qkv)
    vectors = [
        sums,
        grad_b_out,
        grad_b_in,
        grad_b_down,
        grad_gain_one,
        grad_shift_one,
        grad_gain_two,
        grad_shift_two,
    ]
    packed = pack(vectors)
    hidden = [ring.merged(part, high_grad[1], low_grad[1]) for part in (in_grad, down_grad, out_grad)]
    hidden_parts = ring.scatter_columns(hidden, hidden_grad_moves, 2 * hidden_cols + head_cols)
    low_grad = ring.shrink(low_grad, up[1:], hidden_parts[0], packed)
    high_grad = ring.shrink(high_grad, down[1:], hidden_parts[0], packed)
    packed = ring.summed(packed, "dp", (0, 1), low_grad[1], high_grad[1])
    d_qkv = after(d_qkv, low_grad[1], high_grad[1])
    input_grad = d_sum_one + dot_right_t(d_qkv, qkv_w)
    head_parts = ring.scatter_columns(
        (ring.merged(low_grad, input_grad), ring.merged(high_grad, input_grad)), grad_head_moves, 3 * head_cols
    )
    packed = ring.summed(packed, "dp", range(0, ring.dp, 2), head_parts[0])
    packed = ring.summed(packed, "tensor", range(ring.tensor))
    grad_hidden = ring.added(hidden_parts, head_parts[0])
    grad_head = ring.added(head_parts)
    sums, *vectors = unpacked(packed, [vector.shape[0] for vector in vectors])
    query_sum = jnp.concatenate([sums[:HALF], sums[3 * HALF : 4 * HALF]])
    value_sum = jnp.concatenate([sums[2 * HALF : 3 * HALF], sums[5 * HALF :]])
    return (
        layer_out,
        input_grad,
        grad_head[:, :head_cols],
        grad_head[:, head_cols : 2 * head_cols],
        grad_head[:, 2 * head_cols : 3 * head_cols],
        grad_hidden[:, 2 * hidden_cols :].T,
        grad_hidden[:, :hidden_cols],
        grad_hidden[:, hidden_cols : 2 * hidden_cols].T,
        query_sum,
        value_sum,
        *vectors,
    )


def solution(mesh):
    rows = P(("dp", "tensor"), None)
    wide = P("dp", "tensor")
    tall = P("tensor", "dp")
    vectors = (P(),) * 9
    in_specs = (rows, P("dp", None), wide, wide, wide, tall, wide, tall, *vectors, rows)
    out_specs = (rows, rows, wide, wide, wide, tall, wide, tall, *vectors)
    return jax.shard_map(
        functools.partial(on_device, mesh),
        mesh=mesh,
        in_specs=in_specs,
        out_specs=out_specs,
        check_vma=False,
    )
```

```python
import functools

import jax
import jax.numpy as jnp
from jax import lax
from jax.experimental import pallas as pl
from jax.experimental.pallas import tpu as pltpu
from jax.sharding import PartitionSpec as P

D = 768
HD = 64
L = 1024
PAIR = 2 * HD
BLOCK = 256
GRAIN = 128
SIZES = (2, 3, 4, 5, 6, 8)

epsilon = 1e-06
masked_score = -1e30
scale = HD ** (-0.5)
bf16 = jnp.bfloat16
f32 = jnp.float32


def contract(left, right, dims):
    return lax.dot_general(left, right, (dims, ((), ())), preferred_element_type=f32)


def head_lanes(rows, head):
    lane = lax.broadcasted_iota(jnp.int32, (rows, PAIR), 1)
    return (lane // HD) == head


def windows(info_ref, step, body):
    first = info_ref[2 * step]
    need = info_ref[2 * step + 1]
    below = 0
    for size in SIZES:

        @pl.when((need > below) & (need <= size))
        def _():
            start = jnp.minimum(first, L // GRAIN - size) * GRAIN
            body(pl.ds(pl.multiple_of(start, GRAIN), size * GRAIN))

        below = size


def lanes(start):
    return pl.ds(pl.multiple_of(start, PAIR), PAIR)


def stacked(rows):
    zero = jnp.zeros_like(rows)
    return jnp.concatenate(
        [jnp.where(head_lanes(BLOCK, 0), rows, zero), jnp.where(head_lanes(BLOCK, 1), rows, zero)], axis=0
    )


def unstacked(rows):
    return jnp.where(head_lanes(BLOCK, 0), rows[:BLOCK], rows[BLOCK:])


def forward_kernel(info_ref, seg_col_ref, seg_row_ref, qkv_ref, out_ref):
    step = pl.program_id(0)
    rows = pl.ds(pl.multiple_of(step * BLOCK, BLOCK), BLOCK)

    def body(window):
        same = seg_col_ref[...] == seg_row_ref[:, window]
        bias = jnp.where(same, 0.0, masked_score)
        bias = jnp.concatenate([bias, bias], axis=0)

        def one_pair(pair, _):
            base = (pair // HALF_PAIRS * 3 * HALF_PAIRS + pair % HALF_PAIRS) * PAIR
            query = stacked(qkv_ref[rows, lanes(base)] * bf16(scale))
            keys = qkv_ref[window, lanes(base + HALF)]
            values = qkv_ref[window, lanes(base + 2 * HALF)]
            scores = contract(query, keys, ((1,), (1,))) + bias
            top = jnp.max(scores, axis=1, keepdims=True)
            probs = jnp.exp(scores - top)
            total = jnp.sum(probs, axis=1, keepdims=True)
            mixed = contract(probs.astype(bf16), values, ((1,), (0,))) / total
            out_ref[:, lanes(pair * PAIR)] = unstacked(mixed).astype(bf16)
            return 0

        lax.fori_loop(0, PAIRS, one_pair, 0, unroll=3)

    windows(info_ref, step, body)


def backward_kernel(base, info_ref, seg_col_ref, seg_row_ref, qkv_ref, d_ref, out_ref, dk_sum, dv_sum):
    step = pl.program_id(0)
    rows = pl.ds(pl.multiple_of(step * BLOCK, BLOCK), BLOCK)

    @pl.when(step == 0)
    def _():
        dk_sum[...] = jnp.zeros_like(dk_sum)
        dv_sum[...] = jnp.zeros_like(dv_sum)

    def body(window):
        same = seg_col_ref[window, :] == seg_row_ref[...]
        bias = jnp.where(same, 0.0, masked_score)
        bias = jnp.concatenate([bias, bias], axis=1)

        def one_pair(pair, _):
            query = stacked(qkv_ref[rows, lanes(3 * base + pair * PAIR)] * bf16(scale))
            keys = qkv_ref[window, lanes(3 * base + HALF + pair * PAIR)]
            values = qkv_ref[window, lanes(3 * base + 2 * HALF + pair * PAIR)]
            upstream = stacked(d_ref[:, lanes(base + pair * PAIR)])
            scores = contract(keys, query, ((1,), (1,))) + bias
            probs = jnp.exp(scores - jnp.max(scores, axis=0, keepdims=True))
            probs = probs * (1.0 / jnp.sum(probs, axis=0, keepdims=True))
            d_probs = contract(values, upstream, ((1,), (1,)))
            inner = jnp.sum(probs * d_probs, axis=0, keepdims=True)
            d_scores = (probs * (d_probs - inner)).astype(bf16)
            here = lanes(pair * PAIR)
            dk_sum[window, here] += contract(d_scores, query, ((1,), (0,)))
            dv_sum[window, here] += contract(probs.astype(bf16), upstream, ((1,), (0,)))
            dq = contract(d_scores, keys, ((0,), (0,)))
            out_ref[rows, here] = (unstacked(dq) * scale).astype(bf16)
            return 0

        lax.fori_loop(0, HALF_PAIRS, one_pair, 0, unroll=3)

    windows(info_ref, step, body)

    @pl.when(step == pl.num_programs(0) - 1)
    def _():
        out_ref[:, HALF : 2 * HALF] = dk_sum[...].astype(bf16)
        out_ref[:, 2 * HALF :] = dv_sum[...].astype(bf16)


def window_info(segment):
    heads_of = segment.reshape(L // BLOCK, BLOCK)
    first = jnp.sum(segment[None, :] < heads_of[:, :1], axis=1)
    last = jnp.sum(segment[None, :] <= heads_of[:, -1:], axis=1)
    begin = first // GRAIN
    need = (last + GRAIN - 1) // GRAIN - begin
    return jnp.stack([begin, need], axis=1).reshape(-1).astype(jnp.int32)


PAIRS = D // PAIR
HALF = D // 2
HALF_PAIRS = HALF // PAIR


def attend_forward(qkv, segment, info):
    return pl.pallas_call(
        forward_kernel,
        out_shape=jax.ShapeDtypeStruct((L, D), bf16),
        grid_spec=pltpu.PrefetchScalarGridSpec(
            num_scalar_prefetch=1,
            grid=(L // BLOCK,),
            in_specs=[
                pl.BlockSpec((BLOCK, 1), lambda step, info: (step, 0)),
                pl.BlockSpec((1, L), lambda step, info: (0, 0)),
                pl.BlockSpec((L, 3 * D), lambda step, info: (0, 0)),
            ],
            out_specs=pl.BlockSpec((BLOCK, D), lambda step, info: (step, 0)),
        ),
        cost_estimate=pl.CostEstimate(flops=26 * 10**9, transcendentals=0, bytes_accessed=8 * 10**6),
        name="attend_forward",
    )(info, segment.reshape(L, 1), segment.reshape(1, L), qkv)


def attend_backward(qkv, d_mixed, segment, info, half):
    return pl.pallas_call(
        functools.partial(backward_kernel, half * HALF),
        out_shape=jax.ShapeDtypeStruct((L, 3 * HALF), bf16),
        grid_spec=pltpu.PrefetchScalarGridSpec(
            num_scalar_prefetch=1,
            grid=(L // BLOCK,),
            in_specs=[
                pl.BlockSpec((L, 1), lambda step, info: (0, 0)),
                pl.BlockSpec((1, BLOCK), lambda step, info: (0, step)),
                pl.BlockSpec((L, 3 * D), lambda step, info: (0, 0)),
                pl.BlockSpec((BLOCK, D), lambda step, info: (step, 0)),
            ],
            out_specs=pl.BlockSpec((L, 3 * HALF), lambda step, info: (0, 0)),
            scratch_shapes=[pltpu.VMEM((L, HALF), f32), pltpu.VMEM((L, HALF), f32)],
        ),
        cost_estimate=pl.CostEstimate(flops=22 * 10**9, transcendentals=0, bytes_accessed=6 * 10**6),
        name="attend_backward",
    )(info, segment.reshape(L, 1), segment.reshape(1, L), qkv, d_mixed)


def swap(value, axis, size, bit):
    return lax.ppermute(value, axis, [(i, i ^ bit) for i in range(size)])


def partner(value, axis, size, mask):
    return value if mask == 0 else swap(value, axis, size, mask)


def after(value, *others):
    return lax.optimization_barrier((value, *others))[0]


def bits_of(size):
    return [1 << k for k in range(size.bit_length() - 1)]


class Ring:
    def __init__(self, mesh):
        self.dp = mesh.shape["dp"]
        self.tensor = mesh.shape["tensor"]
        self.dp_rank = lax.axis_index("dp")
        self.tensor_rank = lax.axis_index("tensor")

    def outer_bits(self, flip):
        bits = bits_of(self.dp)[1:]
        return bits[::-1] if flip else bits

    def columns_sent(self, shard):
        return [partner(shard, "tensor", self.tensor, mask) for mask in range(self.tensor)]

    def spread_columns(self, pieces, moves, widths):
        rows = pieces[0].shape[0]

        def kernel(rank_ref, *refs):
            ins, outs = refs[: self.tensor], refs[self.tensor :]
            for rank in range(self.tensor):

                @pl.when(rank_ref[0] == rank)
                def _():
                    for mask in range(self.tensor):
                        for source, width, which, place in moves(rank ^ mask):
                            outs[which][:, place : place + width] = ins[mask][:, source : source + width]

        return pl.pallas_call(
            kernel,
            out_shape=[jax.ShapeDtypeStruct((rows, width), pieces[0].dtype) for width in widths],
            in_specs=[pl.BlockSpec(memory_space=pltpu.SMEM)] + [pl.BlockSpec()] * self.tensor,
            name="spread",
        )(self.tensor_rank.reshape(1), *pieces)

    def pick_columns(self, blocks, moves, width):
        rows = blocks[0].shape[0]

        def kernel(rank_ref, *refs):
            ins, outs = refs[: len(blocks)], refs[len(blocks) :]
            for rank in range(self.tensor):

                @pl.when(rank_ref[0] == rank)
                def _():
                    for mask in range(self.tensor):
                        for source, span, which, place in moves(rank ^ mask):
                            value = ins[which][:, place : place + span]
                            outs[mask][:, source : source + span] = value.astype(outs[mask].dtype)

        return pl.pallas_call(
            kernel,
            out_shape=[
                jax.ShapeDtypeStruct((rows, width), bf16 if mask else f32) for mask in range(self.tensor)
            ],
            in_specs=[pl.BlockSpec(memory_space=pltpu.SMEM)] + [pl.BlockSpec()] * len(blocks),
            name="pick",
        )(self.tensor_rank.reshape(1), *blocks)

    def join(self, block, bit, place, *others):
        other = swap(block, "dp", self.dp, bit)
        if others:
            other = after(other, *others)
        upper = (self.dp_rank & bit) != 0
        return jnp.concatenate(
            [jnp.where(upper, other, block), jnp.where(upper, block, other)], axis=place
        )

    def row_axes(self, block):
        return block.reshape((1,) * len(bits_of(self.dp)) + block.shape)

    def grow(self, block, bits, *others):
        for bit in bits:
            block = self.join(block, bit, len(bits_of(self.dp)) - bit.bit_length(), *others)
        return block

    def rows_of(self, block):
        return block.reshape(-1, block.shape[-1])

    def split(self, block, bit):
        if block.ndim == 2:
            count = len(bits_of(self.dp))
            block = block.reshape((2,) * count + (block.shape[0] // self.dp, block.shape[1]))
        place = block.ndim - 2 - bit.bit_length()
        own = (self.dp_rank // bit) % 2
        keep = lax.dynamic_slice_in_dim(block, own, 1, axis=place).astype(f32)
        give = lax.dynamic_slice_in_dim(block, 1 - own, 1, axis=place).astype(bf16)
        return keep, give, swap(give, "dp", self.dp, bit)

    def received(self, parts, *others):
        got = after(parts[2], *others) if others else parts[2]
        return parts[0] + got.astype(f32)

    def shrink(self, parts, bits, *others):
        for bit in bits:
            parts = self.split(self.received(parts, *others), bit)
        return parts

    def merged(self, parts, *others):
        return self.rows_of(self.received(parts, *others))

    def scatter_columns(self, blocks, moves, width):
        result, *sends = self.pick_columns(blocks, moves, width)
        return [result] + [swap(send, "tensor", self.tensor, mask) for mask, send in enumerate(sends, 1)]

    def added(self, parts, *others):
        parts = lax.optimization_barrier((*parts, *others))[: len(parts)]
        return functools.reduce(lambda left, right: left + right.astype(f32), parts)

    def summed(self, value, axis, masks, *others):
        parts = [partner(value, axis, getattr(self, axis), mask) for mask in masks]
        parts = lax.optimization_barrier((*parts, *others))[: len(parts)]
        while len(parts) > 1:
            parts = [left + right for left, right in zip(parts[::2], parts[1::2])]
        return parts[0]


def pack(vectors):
    total = sum(vector.shape[0] for vector in vectors)

    def kernel(*refs):
        row = 0
        for ref in refs[:-1]:
            for start in range(0, ref.shape[1], 128):
                refs[-1][row : row + 1, :] = ref[:, start : start + 128]
                row += 1

    return pl.pallas_call(
        kernel, out_shape=jax.ShapeDtypeStruct((total // 128, 128), f32), name="pack"
    )(*[vector.reshape(1, -1) for vector in vectors])


def projection_bias(query_bias, value_bias):
    def kernel(query_ref, value_ref, out_ref):
        out_ref[...] = jnp.zeros_like(out_ref)
        for half in range(2):
            here = half * HALF
            out_ref[:, 3 * here : 3 * here + HALF] = query_ref[:, here : here + HALF]
            out_ref[:, 3 * here + 2 * HALF : 3 * here + 3 * HALF] = value_ref[:, here : here + HALF]

    return pl.pallas_call(
        kernel, out_shape=jax.ShapeDtypeStruct((1, 3 * D), f32), name="projection_bias"
    )(query_bias.reshape(1, -1), value_bias.reshape(1, -1))


def unpacked(packed, lengths):
    packed, parts, start = packed.reshape(-1), [], 0
    for length in lengths:
        parts.append(packed[start : start + length])
        start += length
    return parts


def dot(left, right):
    return jnp.dot(left, right, preferred_element_type=f32)


def dot_right_t(left, right):
    return jnp.einsum("ik,jk->ij", left, right, preferred_element_type=f32)


def weight_grad(left, right):
    return jnp.einsum("ti,tj->ij", left, right, preferred_element_type=f32).astype(bf16)


def norm_forward(total, gain, shift_by):
    average = jnp.mean(total, axis=-1, keepdims=True)
    centred = total - average
    inverse = lax.rsqrt(jnp.mean(centred * centred, axis=-1, keepdims=True) + epsilon)
    normed = centred * inverse
    return (normed * gain + shift_by, normed, inverse)


def norm_backward(upstream, normed, inverse, gain):
    scaled = upstream * gain
    first_term = jnp.mean(scaled, axis=-1, keepdims=True)
    second_term = jnp.mean(scaled * normed, axis=-1, keepdims=True)
    d_total = inverse * (scaled - first_term - normed * second_term)
    return (d_total, jnp.sum(upstream * normed, axis=0), jnp.sum(upstream, axis=0))


def column_sum(value):
    return jnp.sum(value.astype(f32), axis=0)


def on_device(
    mesh,
    tokens,
    segments,
    w_query,
    w_key,
    w_value,
    w_out,
    w_in,
    w_down,
    b_query,
    b_value,
    b_out,
    b_in,
    b_down,
    gain_one,
    shift_one,
    gain_two,
    shift_two,
    cotangent,
):
    ring = Ring(mesh)
    segment = lax.dynamic_slice_in_dim(segments, ring.tensor_rank, 1, 0).reshape(L)
    info = window_info(segment)
    head_cols = w_query.shape[1]
    hidden_cols = w_in.shape[1]
    halves = ring.tensor // 2

    def head_moves(rank, kinds=4):
        for kind in range(kinds):
            place = kind * HALF + rank % halves * head_cols
            yield kind * head_cols, head_cols, rank // halves, place

    grad_head_moves = functools.partial(head_moves, kinds=3)

    def hidden_moves(rank):
        for kind in range(2):
            yield kind * hidden_cols, hidden_cols, kind, rank * hidden_cols

    def hidden_grad_moves(rank):
        yield from hidden_moves(rank)
        yield 2 * hidden_cols, head_cols, 2, rank * head_cols

    up, down = ring.outer_bits(False), ring.outer_bits(True)
    head_shard = jnp.concatenate([w_query, w_key, w_value, w_out.T], axis=1)
    low, high = ring.spread_columns(ring.columns_sent(head_shard), head_moves, (4 * HALF, 4 * HALF))
    hidden_shard = after(jnp.concatenate([w_in, w_down.T], axis=1), low, high)
    hidden_pieces = ring.columns_sent(hidden_shard)
    low = ring.grow(ring.row_axes(low), up[:-1], hidden_pieces[1])
    high = ring.grow(ring.row_axes(high), down[:-1], hidden_pieces[1])
    low = ring.grow(low, up[-1:], *hidden_pieces[2:])
    high = ring.grow(high, down[-1:], *hidden_pieces[2:])
    in_part, down_part = ring.spread_columns(hidden_pieces, hidden_moves, (ring.tensor * hidden_cols,) * 2)
    low_w = ring.rows_of(ring.grow(low, [1], in_part, down_part))
    high_w = ring.rows_of(ring.grow(high, [1], in_part, down_part))
    qkv_w = jnp.concatenate([low_w[:, : 3 * HALF], high_w[:, : 3 * HALF]], axis=1)
    out_t = jnp.concatenate([low_w[:, 3 * HALF :], high_w[:, 3 * HALF :]], axis=1)

    qkv = (dot(tokens, qkv_w) + projection_bias(b_query, b_value)).astype(bf16)
    in_part = ring.grow(ring.row_axes(in_part), up[:-1], qkv)
    down_part = ring.grow(ring.row_axes(down_part), down[:-1], qkv)
    qkv = after(qkv, in_part, down_part)
    mixed = attend_forward(qkv, segment, info)
    in_part = ring.grow(in_part, up[-1:], mixed)
    down_part = ring.grow(down_part, down[-1:], mixed)
    mixed = after(mixed, in_part, down_part)
    in_w = ring.rows_of(ring.grow(in_part, [1]))
    down_t = ring.rows_of(ring.grow(down_part, [1]))
    branch = dot_right_t(mixed, out_t) + b_out
    first, normed_one, inverse_one = norm_forward(tokens.astype(f32) + branch, gain_one, shift_one)
    first_low = first.astype(bf16)
    inner = dot(first_low, in_w) + b_in
    half = 0.5 * (1.0 + lax.erf(inner * (0.5**0.5)))
    active = (inner * half).astype(bf16)
    slope = (half + inner * jnp.exp(-0.5 * inner * inner) * ((0.5 / jnp.pi) ** 0.5)).astype(bf16)
    active, slope = lax.optimization_barrier((active, slope))
    branch_two = dot_right_t(active, down_t) + b_down
    second, normed_two, inverse_two = norm_forward(first + branch_two, gain_two, shift_two)
    layer_out = second.astype(bf16)

    d_sum_two, grad_gain_two, grad_shift_two = norm_backward(
        cotangent.astype(f32), normed_two, inverse_two, gain_two
    )
    grad_branch_two = d_sum_two.astype(bf16)
    grad_b_down = column_sum(grad_branch_two)
    up, down = up[::-1], down[::-1]
    down_grad = ring.split(weight_grad(grad_branch_two, active), 1)
    grad_branch_two = after(grad_branch_two, down_grad[1])
    d_inner = (dot(grad_branch_two, down_t) * slope.astype(f32)).astype(bf16)
    grad_b_in = column_sum(d_inner)
    down_grad = ring.shrink(down_grad, down[:-1])
    d_inner = after(d_inner, down_grad[1])
    in_grad = ring.split(weight_grad(first_low, d_inner), 1)
    d_inner = after(d_inner, in_grad[1])
    d_first = d_sum_two + dot_right_t(d_inner, in_w)
    d_sum_one, grad_gain_one, grad_shift_one = norm_backward(
        d_first, normed_one, inverse_one, gain_one
    )
    grad_branch = d_sum_one.astype(bf16)
    grad_b_out = column_sum(grad_branch)
    in_grad = ring.shrink(in_grad, up[:-1])
    grad_branch = after(grad_branch, in_grad[1])
    out_grad = ring.split(weight_grad(grad_branch, mixed), 1)
    grad_branch = after(grad_branch, out_grad[1])
    d_mixed = dot(grad_branch, out_t).astype(bf16)
    d_low = attend_backward(qkv, d_mixed, segment, info, 0)
    down_grad = ring.shrink(down_grad, down[-1:], d_low)
    in_grad = ring.shrink(in_grad, up[-1:], d_low)
    d_low = after(d_low, down_grad[1], in_grad[1])
    low_grad = ring.split(weight_grad(tokens, d_low), 1)
    out_grad = ring.shrink(out_grad, up[:-1], d_low)
    low_sum = column_sum(d_low)
    d_mixed = after(d_mixed, out_grad[1], low_grad[1], low_sum)
    d_high = attend_backward(qkv, d_mixed, segment, info, 1)
    high_grad = ring.split(weight_grad(tokens, d_high), 1)
    low_grad = ring.shrink(low_grad, up[:-1], high_grad[1])
    out_grad = ring.shrink(out_grad, up[-1:], high_grad[1])
    high_grad = ring.shrink(high_grad, down[:1])
    d_qkv = jnp.concatenate([d_low, d_high], axis=1)
    vectors = [
        low_sum,
        column_sum(d_high),
        grad_b_out,
        grad_b_in,
        grad_b_down,
        grad_gain_one,
        grad_shift_one,
        grad_gain_two,
        grad_shift_two,
    ]
    packed = pack(vectors)
    hidden = [ring.merged(part, high_grad[1], low_grad[1]) for part in (in_grad, down_grad, out_grad)]
    hidden_parts = ring.scatter_columns(hidden, hidden_grad_moves, 2 * hidden_cols + head_cols)
    low_grad = ring.shrink(low_grad, up[1:], hidden_parts[0], packed)
    high_grad = ring.shrink(high_grad, down[1:], hidden_parts[0], packed)
    packed = ring.summed(packed, "dp", (0, 1), low_grad[1], high_grad[1])
    d_qkv = after(d_qkv, low_grad[1], high_grad[1])
    input_grad = d_sum_one + dot_right_t(d_qkv, qkv_w)
    head_parts = ring.scatter_columns(
        (ring.merged(low_grad, input_grad), ring.merged(high_grad, input_grad)), grad_head_moves, 3 * head_cols
    )
    packed = ring.summed(packed, "dp", range(0, ring.dp, 2), head_parts[0])
    packed = ring.summed(packed, "tensor", range(ring.tensor))
    grad_hidden = ring.added(hidden_parts, head_parts[0])
    grad_head = ring.added(head_parts)
    low_sum, high_sum, *vectors = unpacked(packed, [vector.shape[0] for vector in vectors])
    query_sum = jnp.concatenate([low_sum[:HALF], high_sum[:HALF]])
    value_sum = jnp.concatenate([low_sum[2 * HALF :], high_sum[2 * HALF :]])
    return (
        layer_out,
        input_grad,
        grad_head[:, :head_cols],
        grad_head[:, head_cols : 2 * head_cols],
        grad_head[:, 2 * head_cols : 3 * head_cols],
        grad_hidden[:, 2 * hidden_cols :].T,
        grad_hidden[:, :hidden_cols],
        grad_hidden[:, hidden_cols : 2 * hidden_cols].T,
        query_sum,
        value_sum,
        *vectors,
    )


def solution(mesh):
    rows = P(("dp", "tensor"), None)
    wide = P("dp", "tensor")
    tall = P("tensor", "dp")
    vectors = (P(),) * 9
    in_specs = (rows, P("dp", None), wide, wide, wide, tall, wide, tall, *vectors, rows)
    out_specs = (rows, rows, wide, wide, wide, tall, wide, tall, *vectors)
    return jax.shard_map(
        functools.partial(on_device, mesh),
        mesh=mesh,
        in_specs=in_specs,
        out_specs=out_specs,
        check_vma=False,
    )
```
